512 devices in a mesh: seq: 64 (over z_hi, y, x), mp: 8 (over z_lo, core).
Axes of the slice: x: 4, y: 8, z: 8 (z_hi: 2, z_lo: 4; z = z_hi * 4 + z_lo), core: 2. Of those that a mesh axis runs over, the one named last changes fastest.
Arguments:
- stream_q: bfloat16 [16384, 2048], P('seq', 'mp'), may hold values from -6 to 6
- stream_k: bfloat16 [16384, 2048], P('seq', 'mp'), may hold values from -6 to 6
- stream_v: bfloat16 [16384, 2048], P('seq', 'mp'), may hold values from -6 to 6
- filter_taps: float32 [2048, 128], P('mp'), may hold values from -4 to 4
- decay_rate: float32 [2048], P('mp'), may hold values from 0.004 to 0.15
- residual: bfloat16 [16384, 2048], P('seq', 'mp'), may hold values from -6 to 6
- norm_gain: float32 [2048], P('mp'), may hold values from 0.5 to 1.5
- queries: bfloat16 [16384, 2048], P('seq', 'mp'), may hold values from -50 to 50
- keys: bfloat16 [16384, 2048], P('seq', 'mp'), may hold values from -6 to 6
Outputs:
- normed: bfloat16 [16384, 2048], P('seq', 'mp')
- attended: bfloat16 [16384, 2048], P('seq', 'mp')
The draws below stay inside these ranges and needn't reach their ends.
All inputs are finite; a program needn't handle non-finite values.
Results may differ from the reference program's by a relative error of at most 0.0061.
Values may be sent and summed in bfloat16 or wider, within the bound.
A program may use at most 128 MiB of HBM per device.

```python
import math
import jax
import jax.numpy as jnp
from jax import lax

CH = 2048
HD = 128
TAPS = 128
TOKENS = 16384


def draw_pair(key):
    base = jax.random.fold_in(key, 1234)
    key_q, key_k = jax.random.split(base, 2)
    key_field = jnp.clip(jax.random.normal(key_k, (TOKENS, CH), jnp.float32), -6.0, 6.0)
    query_field = 2.5 * jnp.clip(jax.random.normal(key_q, (TOKENS, CH), jnp.float32), -6.0, 6.0)
    return (query_field, key_field)


def draw_queries(key, part):
    return draw_pair(key)[0].astype(jnp.bfloat16)


def draw_keys(key, part):
    return draw_pair(key)[1].astype(jnp.bfloat16)


def shard_levels(key, dims, cuts, least, top_value):
    gain = 1.0
    for dim, blocks in cuts:
        heights = jax.random.uniform(jax.random.fold_in(jax.random.fold_in(key, 6), dim), (blocks,), jnp.float32, least / len(cuts), top_value / len(cuts))
        gain = gain * jnp.repeat(jnp.exp(heights), dims[dim] // blocks).reshape((-1,) + (1,) * (len(dims) - 1 - dim))
    return gain


def centred(own_key, shape, spread, limit, cuts=(), held_as=jnp.bfloat16):
    array = spread * jax.random.normal(own_key, shape, jnp.float32)
    if cuts:
        array = array * shard_levels(own_key, shape, cuts, -0.22, 0.18)
    return jnp.clip(array, -limit, limit).astype(held_as)


def setup_inputs(seed: int = 0) -> dict:
    splits = jax.random.split(jax.random.key(seed), 10)
    return {
        "stream_q": centred(splits[0], (TOKENS, CH), 1.0, 6.0, ((0, 64), (1, 8))),
        "stream_k": centred(splits[1], (TOKENS, CH), 1.0, 6.0, ((0, 64), (1, 8))),
        "stream_v": centred(splits[2], (TOKENS, CH), 1.0, 6.0, ((0, 64), (1, 8))),
        "filter_taps": centred(splits[3], (CH, TAPS), 0.3, 4.0, ((0, 8),), jnp.float32),
        "decay_rate": jnp.clip(jnp.exp(math.log(0.15) - 3.624341 * jax.random.uniform(splits[4], (CH,), jnp.float32) ** shard_levels(splits[4], (CH,), ((0, 8),), -0.2, 0.2)), 0.004, 0.15),
        "residual": centred(splits[5], (TOKENS, CH), 1.0, 6.0, ((0, 64), (1, 8))),
        "norm_gain": jnp.clip(1.0 + 0.1 * jax.random.normal(splits[6], (CH,), jnp.float32), 0.5, 1.5),
        "queries": draw_queries(jax.random.fold_in(splits[9], 71), 0),
        "keys": draw_keys(jax.random.fold_in(splits[9], 71), 0),
    }


norm_eps = 1e-06
neg_large = -1e+30

def causal_filter(extended, kernel):
    tap_count = kernel.shape[1]
    row_count = extended.shape[0] - (tap_count - 1)

    def add_tap(total, tap):
        start = (tap_count - 1 - tap).astype(jnp.int32)
        piece = lax.dynamic_slice_in_dim(extended, start, row_count, 0)
        coeff = lax.dynamic_slice_in_dim(kernel, tap.astype(jnp.int32), 1, 1)[:, 0]
        return (total + piece * coeff[None, :], None)
    initial = jnp.zeros((row_count, extended.shape[1]), extended.dtype)
    total, _ = lax.scan(add_tap, initial, jnp.arange(tap_count).astype(jnp.int32))
    return total

def reference(stream_q, stream_k, stream_v, filter_taps, decay_rate, residual, norm_gain, queries, keys):
    gated_input = (stream_k.astype(jnp.float32) * stream_v.astype(jnp.float32)).astype(jnp.bfloat16)
    tap_index = jnp.arange(TAPS).astype(jnp.float32)
    kernel = filter_taps * jnp.exp(-decay_rate[:, None] * tap_index[None, :])
    extended = jnp.concatenate([jnp.zeros((TAPS - 1, CH), jnp.float32), gated_input.astype(jnp.float32)], axis=0)
    filtered = causal_filter(extended, kernel)
    hyena_out = (stream_q.astype(jnp.float32) * filtered).astype(jnp.bfloat16)
    summed = residual.astype(jnp.float32) + hyena_out.astype(jnp.float32)
    mean_square = lax.optimization_barrier(jnp.sum(summed * summed, axis=1)) / CH
    normed = (summed * lax.rsqrt(mean_square + norm_eps)[:, None] * norm_gain[None, :]).astype(jnp.bfloat16)
    head_count = CH // HD
    score_scale = 1.0 / math.sqrt(HD)
    query_heads = queries.reshape(TOKENS, head_count, HD).transpose(1, 0, 2)
    key_heads = keys.reshape(TOKENS, head_count, HD).transpose(1, 0, 2)
    value_heads = normed.reshape(TOKENS, head_count, HD).transpose(1, 0, 2)
    block_rows = min(TOKENS, 1024)
    pieces_out = []
    for block_index in range(TOKENS // block_rows):
        key_end = (block_index + 1) * block_rows
        query_pos = block_index * block_rows + jnp.arange(block_rows).astype(jnp.int32)
        key_pos = jnp.arange(key_end).astype(jnp.int32)
        visible = key_pos[None, :] <= query_pos[:, None]

        def one_head(operands):
            query_head, key_head, value_head = operands
            score = jnp.dot(query_head, key_head.T, preferred_element_type=jnp.float32) * score_scale
            score = jnp.where(visible, score, neg_large)
            row_max = lax.optimization_barrier(jnp.max(score, axis=1, keepdims=True))
            weight = jnp.where(visible, jnp.exp(score - row_max), 0.0)
            denominator = lax.optimization_barrier(jnp.sum(weight, axis=1))
            numerator = jnp.dot(weight.astype(jnp.bfloat16), value_head, preferred_element_type=jnp.float32)
            return numerator / denominator[:, None]
        head_out = lax.map(one_head, (query_heads[:, block_index * block_rows:key_end], key_heads[:, :key_end], value_heads[:, :key_end]))
        pieces_out.append(head_out.transpose(1, 0, 2).reshape(block_rows, CH))
    attended = jnp.concatenate(pieces_out, axis=0).astype(jnp.bfloat16)
    return (normed, attended)
```

```python
import functools
import math

import jax
import jax.numpy as jnp
from jax import lax
from jax.experimental import pallas as pl
from jax.experimental.pallas import tpu as pltpu
from jax.sharding import Mesh, PartitionSpec as P

HD = 128
ROWS = 256
WIDTH = 256
TAPS = 128
HEADS = WIDTH // HD
EPS = 1e-06
LOW = -1e30
SCALE2 = math.log2(math.e) / math.sqrt(HD)
MESH = pl.DeviceIdType.MESH
AXES = ("zh", "y", "x", "mp")


def body(
    sizes,
    sq_ref, sk_ref, sv_ref, taps_ref, decay_ref, res_ref, gain_ref, q_ref, k_ref,
    normed_ref, out_ref,
    halo_k, halo_v, shifted, taps_t, filtered, squares,
    q_all, k_all, v_all, part, part_in, stat, stat_in, m_ref, l_ref, acc_ref,
    halo_send, halo_recv, sq_send, sq_recv, q_send, q_recv,
    k_send, k_recv, v_send, v_recv, p_send, p_recv, s_send, s_recv,
):
    nz, ny, nx, nm = sizes
    zh, y, x, mp = (lax.axis_index(name) for name in AXES)
    seq = (zh * ny + y) * nx + x
    mine = zh * nx + x
    other = (1 - zh) * nx + x
    total_seq = nz * ny * nx

    def at_seq(s):
        return (s // (ny * nx), lax.rem(s // nx, ny), lax.rem(s, nx), mp)

    def at_y(p):
        return (zh, p, x, mp)

    def at_x(p):
        return (zh, y, p, mp)

    def at_mp(p):
        return (zh, y, x, p)

    partner = (1 - zh, y, x, mp)
    following = at_seq(lax.rem(seq + 1, total_seq))
    previous = at_seq(lax.rem(seq + total_seq - 1, total_seq))

    def remote(src, dst, send, recv, device):
        return pltpu.make_async_remote_copy(
            src_ref=src, dst_ref=dst, send_sem=send, recv_sem=recv,
            device_id=device, device_id_type=MESH,
        )

    barrier = pltpu.get_barrier_semaphore()
    greeted = [previous, partner]
    greeted += [at_y(lax.rem(y + d, ny)) for d in range(1, ny)]
    greeted += [at_x(lax.rem(x + d, nx)) for d in range(1, nx)]
    greeted += [at_mp(lax.rem(mp + d, nm)) for d in range(1, nm)]
    for device in greeted:
        pl.semaphore_signal(barrier, inc=1, device_id=device, device_id_type=MESH)
    pl.semaphore_wait(barrier, len(greeted))

    tail = pl.ds(ROWS - TAPS, TAPS)
    halos = [
        remote(sk_ref.at[tail], halo_k, halo_send.at[0], halo_recv.at[0], following),
        remote(sv_ref.at[tail], halo_v, halo_send.at[1], halo_recv.at[1], following),
    ]
    for copy in halos:
        copy.start()

    sends = []

    def spread(src, table, send, recv, first, slot):
        for d in range(1, nx):
            copy = remote(
                src, table.at[slot], send.at[first + d], recv.at[slot],
                at_x(lax.rem(x + d, nx)),
            )
            copy.start()
            sends.append(copy)

    def across(src, table, send, recv):
        copy = remote(src, table.at[mine], send.at[0], recv.at[mine], partner)
        copy.start()
        sends.append(copy)

    def arrived(table, send, recv, slot):
        remote(table.at[slot], table.at[slot], send.at[0], recv.at[slot], partner).wait_recv()

    across(k_ref, k_all, k_send, k_recv)
    spread(k_ref, k_all, k_send, k_recv, 0, mine)
    for d in range(1, ny):
        copy = remote(
            q_ref, q_all.at[y], q_send.at[d], q_recv.at[y], at_y(lax.rem(y + d, ny))
        )
        copy.start()
        sends.append(copy)
    q_all[y] = q_ref[...]
    k_all[mine] = k_ref[...]

    steps = lax.broadcasted_iota(jnp.int32, (TAPS, WIDTH), 0).astype(jnp.float32)
    taps_t[...] = taps_ref[...].T * jnp.exp(-decay_ref[...] * steps)

    def gate(a, b):
        return (a.astype(jnp.float32) * b.astype(jnp.float32)).astype(jnp.bfloat16).astype(jnp.float32)

    own_gated = gate(sk_ref[...], sv_ref[...])
    for r in range(8):
        shifted[r, TAPS + r : TAPS + r + ROWS, :] = own_gated
    for copy in halos:
        copy.wait()
    edge = gate(halo_k[...], halo_v[...])
    edge = jnp.where(seq > 0, edge, 0.0)
    for r in range(8):
        shifted[r, r : r + TAPS, :] = edge

    arrived(k_all, k_send, k_recv, other)
    spread(k_all.at[other], k_all, k_send, k_recv, nx - 1, other)

    chunk = 64

    def filter_chunk(c, _):
        base = TAPS + c * chunk

        def eight(j, total):
            coeff = taps_t[pl.ds(pl.multiple_of(j * 8, 8), 8), :]
            rows = pl.ds(pl.multiple_of(base - j * 8, 8), chunk)
            for r in range(8):
                total = total + shifted[r, rows, :] * coeff[r : r + 1, :]
            return total

        total = lax.fori_loop(0, TAPS // 8, eight, jnp.zeros((chunk, WIDTH), jnp.float32))
        here = pl.ds(pl.multiple_of(c * chunk, chunk), chunk)
        hyena = (sq_ref[here, :].astype(jnp.float32) * total).astype(jnp.bfloat16)
        filtered[here, :] = res_ref[here, :].astype(jnp.float32) + hyena.astype(jnp.float32)
        return 0

    lax.fori_loop(0, ROWS // chunk, filter_chunk, 0)
    summed = filtered[...]
    own_square = jnp.sum(summed * summed, axis=1, keepdims=True)
    squares[mp] = jnp.broadcast_to(own_square, (ROWS, 128)).T[:8]
    for d in range(1, nm):
        copy = remote(
            squares.at[mp], squares.at[mp], sq_send.at[d], sq_recv.at[mp],
            at_mp(lax.rem(mp + d, nm)),
        )
        copy.start()
        sends.append(copy)
    for d in range(1, nm):
        source = lax.rem(mp + d, nm)
        remote(
            squares.at[source], squares.at[source], sq_send.at[d], sq_recv.at[source],
            at_mp(source),
        ).wait_recv()
    square = squares[0]
    for i in range(1, nm):
        square = square + squares[i]
    inverse = lax.rsqrt(square / (nm * WIDTH) + EPS)
    inverse = jnp.concatenate([inverse] * 16, axis=0).T
    inverse = jnp.concatenate([inverse] * (WIDTH // 128), axis=1)
    normed = (filtered[...] * inverse * gain_ref[...]).astype(jnp.bfloat16)
    normed_ref[...] = normed
    v_all[mine] = normed
    across(v_all.at[mine], v_all, v_send, v_recv)
    spread(v_all.at[mine], v_all, v_send, v_recv, 0, mine)
    arrived(v_all, v_send, v_recv, other)
    spread(v_all.at[other], v_all, v_send, v_recv, nx - 1, other)
    for d in range(1, ny):
        source = lax.rem(y + d, ny)
        remote(
            q_all.at[source], q_all.at[source], q_send.at[d], q_recv.at[source], at_y(source)
        ).wait_recv()
    for d in range(1, nx):
        column = lax.rem(x + d, nx)
        for z in range(nz):
            arrived(k_all, k_send, k_recv, z * nx + column)
            arrived(v_all, v_send, v_recv, z * nx + column)

    def tile(h, q_slot, slot, masked):
        lanes = slice(h * HD, (h + 1) * HD)
        score = lax.dot_general(
            q_all[q_slot, :, lanes], k_all[slot, :, lanes], (((1,), (1,)), ((), ())),
            preferred_element_type=jnp.float32,
        ) * SCALE2
        if masked:
            row = lax.broadcasted_iota(jnp.int32, (ROWS, ROWS), 0)
            col = lax.broadcasted_iota(jnp.int32, (ROWS, ROWS), 1)
            score = jnp.where(col <= row, score, LOW)
        before = m_ref[h]
        now = jnp.maximum(before, jnp.max(score, axis=1, keepdims=True))
        m_ref[h] = now
        weight = jnp.exp2(score - jnp.concatenate([now] * (ROWS // 128), axis=1))
        if masked:
            weight = jnp.where(col <= row, weight, 0.0)
        factor = jnp.exp2(before - now)
        lane_sum = weight[:, :128]
        for i in range(1, ROWS // 128):
            lane_sum = lane_sum + weight[:, i * 128 : (i + 1) * 128]
        l_ref[h] = l_ref[h] * factor + lane_sum
        acc_ref[h] = acc_ref[h] * factor + jnp.dot(
            weight.astype(jnp.bfloat16), v_all[slot, :, lanes],
            preferred_element_type=jnp.float32,
        )

    def query_block(i, _):
        q_slot = lax.rem(y + 1 + i, ny)
        is_own = i == ny - 1
        m_ref[...] = jnp.full_like(m_ref, LOW)
        l_ref[...] = jnp.zeros_like(l_ref)
        acc_ref[...] = jnp.zeros_like(acc_ref)
        inside = jnp.where(q_slot > y, nx, jnp.where(is_own, x, 0))
        count = zh * nx + inside

        def step(slot, carry):
            for h in range(HEADS):
                tile(h, q_slot, slot, False)
            return carry

        lax.fori_loop(0, count, step, 0)

        @pl.when(is_own)
        def _():
            for h in range(HEADS):
                tile(h, q_slot, mine, True)

        logs = []
        for h in range(HEADS):
            amount = jnp.sum(l_ref[h], axis=1, keepdims=True)
            amount = jnp.where(amount > 0.0, amount, 1.0)
            part[q_slot, :, h * HD : (h + 1) * HD] = (acc_ref[h] / amount).astype(jnp.bfloat16)
            logs.append(m_ref[h] + jnp.log2(amount))
        lane = lax.broadcasted_iota(jnp.int32, (ROWS, 128), 1)
        stat[q_slot] = jnp.where(lane == 0, logs[0], logs[1]).T[:8]

        @pl.when(jnp.logical_not(is_own))
        def _():
            remote(
                part.at[q_slot], part_in.at[y], p_send.at[q_slot], p_recv.at[y], at_y(q_slot)
            ).start()
            remote(
                stat.at[q_slot], stat_in.at[y], s_send.at[q_slot], s_recv.at[y], at_y(q_slot)
            ).start()

        return 0

    lax.fori_loop(0, ny, query_block, 0)

    for d in range(1, ny):
        source = lax.rem(y + d, ny)
        last = remote(
            part.at[source], part_in.at[source], p_send.at[source], p_recv.at[source],
            at_y(source),
        )
        last.wait()
        last = remote(
            stat.at[source], stat_in.at[source], s_send.at[source], s_recv.at[source],
            at_y(source),
        )
        last.wait()

    stats = [stat[y]] + [stat_in[lax.rem(y + d, ny)] for d in range(1, ny)]
    top = functools.reduce(jnp.maximum, stats)
    raised = [jnp.exp2(s - top) for s in stats]
    norm = functools.reduce(jnp.add, raised)
    share = jnp.concatenate([e / norm for e in raised], axis=0)
    if ny < 16:
        share = jnp.concatenate([share, jnp.zeros((128 - 8 * ny, ROWS), jnp.float32)], axis=0)
    share = share.T
    for h in range(HEADS):
        lanes = slice(h * HD, (h + 1) * HD)
        total = share[:, h : h + 1] * part[y, :, lanes].astype(jnp.float32)
        for d in range(1, ny):
            piece = part_in[lax.rem(y + d, ny), :, lanes].astype(jnp.float32)
            total = total + share[:, d * 8 + h : d * 8 + h + 1] * piece
        out_ref[:, lanes] = total.astype(jnp.bfloat16)

    for copy in sends:
        copy.wait_send()


def build(mesh, sizes):
    nz, ny, nx, nm = sizes
    group = nz * nx

    def local(stream_q, stream_k, stream_v, taps, decay, residual, gain, queries, keys):
        block = jax.ShapeDtypeStruct((ROWS, WIDTH), jnp.bfloat16)
        bf, f32 = jnp.bfloat16, jnp.float32
        vmem = pltpu.VMEM
        dma = pltpu.SemaphoreType.DMA
        return pl.pallas_call(
            functools.partial(body, sizes),
            out_shape=(block, block),
            in_specs=[pl.BlockSpec(memory_space=pltpu.VMEM)] * 9,
            out_specs=(pl.BlockSpec(memory_space=pltpu.VMEM),) * 2,
            scratch_shapes=[
                vmem((TAPS, WIDTH), bf), vmem((TAPS, WIDTH), bf),
                vmem((8, TAPS + ROWS + 8, WIDTH), f32), vmem((TAPS, WIDTH), f32),
                vmem((ROWS, WIDTH), f32), vmem((nm, 8, ROWS), f32),
                vmem((ny, ROWS, WIDTH), bf), vmem((group, ROWS, WIDTH), bf),
                vmem((group, ROWS, WIDTH), bf), vmem((ny, ROWS, WIDTH), bf),
                vmem((ny, ROWS, WIDTH), bf), vmem((ny, 8, ROWS), f32), vmem((ny, 8, ROWS), f32),
                vmem((HEADS, ROWS, 128), f32), vmem((HEADS, ROWS, 128), f32),
                vmem((HEADS, ROWS, HD), f32),
                dma((2,)), dma((2,)), dma((nm,)), dma((nm,)), dma((ny,)), dma((ny,)),
                dma((2 * nx,)), dma((group,)), dma((2 * nx,)), dma((group,)),
                dma((ny,)), dma((ny,)), dma((ny,)), dma((ny,)),
            ],
            compiler_params=pltpu.CompilerParams(
                collective_id=0, has_side_effects=True, vmem_limit_bytes=60 * 1024 * 1024
            ),
        )(
            stream_q, stream_k, stream_v, taps, decay.reshape(1, WIDTH), residual,
            gain.reshape(1, WIDTH), queries, keys,
        )

    inner = Mesh(mesh.devices.reshape(sizes), AXES)
    rows = ("zh", "y", "x")
    array = P(rows, "mp")
    return jax.shard_map(
        local, mesh=inner,
        in_specs=(array, array, array, P("mp", None), P("mp"), array, P("mp"), array, array),
        out_specs=(array, array), check_vma=False,
    )


def solution(mesh):
    seq, nm = mesh.shape["seq"], mesh.shape["mp"]
    return build(mesh, (2, seq // 8, 4, nm))
```

```python
import functools
import math

import jax
import jax.numpy as jnp
from jax import lax
from jax.experimental import pallas as pl
from jax.experimental.pallas import tpu as pltpu
from jax.sharding import Mesh, PartitionSpec as P

HD = 128
ROWS = 256
WIDTH = 256
TAPS = 128
HEADS = WIDTH // HD
EPS = 1e-06
LOW = -1e30
SCALE2 = math.log2(math.e) / math.sqrt(HD)
MESH = pl.DeviceIdType.MESH
AXES = ("zh", "y", "x", "mp")


def body(
    sizes,
    sq_ref, sk_ref, sv_ref, taps_ref, decay_ref, res_ref, gain_ref, q_ref, k_ref,
    normed_ref, out_ref,
    halo_k, halo_v, shifted, taps_t, filtered, squares,
    q_all, k_all, v_all, part, part_in, stat, stat_in, m_ref, l_ref, acc_ref,
    halo_send, halo_recv, sq_send, sq_recv, q_send, q_recv,
    k_send, k_recv, v_send, v_recv, p_send, p_recv, s_send, s_recv,
):
    nz, ny, nx, nm = sizes
    zh, y, x, mp = (lax.axis_index(name) for name in AXES)
    seq = (zh * ny + y) * nx + x
    mine = zh * nx + x
    other = (1 - zh) * nx + x
    total_seq = nz * ny * nx

    def at_seq(s):
        return (s // (ny * nx), lax.rem(s // nx, ny), lax.rem(s, nx), mp)

    def at_y(p):
        return (zh, p, x, mp)

    def at_x(p):
        return (zh, y, p, mp)

    def at_mp(p):
        return (zh, y, x, p)

    partner = (1 - zh, y, x, mp)
    following = at_seq(lax.rem(seq + 1, total_seq))
    previous = at_seq(lax.rem(seq + total_seq - 1, total_seq))

    def remote(src, dst, send, recv, device):
        return pltpu.make_async_remote_copy(
            src_ref=src, dst_ref=dst, send_sem=send, recv_sem=recv,
            device_id=device, device_id_type=MESH,
        )

    barrier = pltpu.get_barrier_semaphore()
    greeted = [previous, partner]
    greeted += [at_y(lax.rem(y + d, ny)) for d in range(1, ny)]
    greeted += [at_x(lax.rem(x + d, nx)) for d in range(1, nx)]
    greeted += [at_mp(lax.rem(mp + d, nm)) for d in range(1, nm)]
    for device in greeted:
        pl.semaphore_signal(barrier, inc=1, device_id=device, device_id_type=MESH)
    pl.semaphore_wait(barrier, len(greeted))

    tail = pl.ds(ROWS - TAPS, TAPS)
    halos = [
        remote(sk_ref.at[tail], halo_k, halo_send.at[0], halo_recv.at[0], following),
        remote(sv_ref.at[tail], halo_v, halo_send.at[1], halo_recv.at[1], following),
    ]
    for copy in halos:
        copy.start()

    sends = []

    left, right = lax.rem(x + nx - 1, nx), lax.rem(x + 1, nx)
    halves = (pl.ds(0, ROWS // 2), pl.ds(ROWS // 2, ROWS // 2))

    def spread(src, table, send, recv, half, act="start"):
        slot = (zh if half == 0 else 1 - zh) * nx + x
        for kind, target in ((0, right), (1, left)):
            n = half * 4 + kind
            copy = remote(src, table.at[slot], send.at[n], recv.at[n], at_x(target))
            getattr(copy, act)()

    def forward(table, send, recv, half, act="start"):
        base = (zh if half == 0 else 1 - zh) * nx
        for kind, target, column in ((0, right, left), (1, left, right)):
            n = half * 4 + kind
            piece = table.at[base + column]
            if act == "start":
                remote(piece, piece, send.at[n], recv.at[n], at_x(target)).wait_recv()
            piece = piece.at[halves[kind]]
            copy = remote(piece, piece, send.at[n + 2], recv.at[n + 2], at_x(target))
            getattr(copy, act)()

    def finish(table, send, recv, half):
        far = (zh if half == 0 else 1 - zh) * nx + lax.rem(x + 2, nx)
        for kind in range(2):
            n = half * 4 + kind + 2
            piece = table.at[far].at[halves[kind]]
            remote(piece, piece, send.at[n], recv.at[n], at_x(left)).wait_recv()

    def across(src, table, send, recv):
        return remote(src, table.at[mine], send.at[8], recv.at[8], partner)

    def arrived(table, send, recv):
        remote(table.at[other], table.at[other], send.at[8], recv.at[8], partner).wait_recv()

    gathers = ((k_all, k_send, k_recv), (v_all, v_send, v_recv))

    @pl.when(zh == 0)
    def _():
        across(k_ref, k_all, k_send, k_recv).start()

    spread(k_ref, k_all, k_send, k_recv, 0)
    for d in range(1, ny):
        copy = remote(
            q_ref, q_all.at[y], q_send.at[d], q_recv.at[y], at_y(lax.rem(y + d, ny))
        )
        copy.start()
        sends.append(copy)
    q_all[y] = q_ref[...]
    k_all[mine] = k_ref[...]

    steps = lax.broadcasted_iota(jnp.int32, (TAPS, WIDTH), 0).astype(jnp.float32)
    taps_t[...] = taps_ref[...].T * jnp.exp(-decay_ref[...] * steps)

    def gate(a, b):
        return (a.astype(jnp.float32) * b.astype(jnp.float32)).astype(jnp.bfloat16).astype(jnp.float32)

    own_gated = gate(sk_ref[...], sv_ref[...])
    for r in range(8):
        shifted[r, TAPS + r : TAPS + r + ROWS, :] = own_gated
    for copy in halos:
        copy.wait()
    edge = gate(halo_k[...], halo_v[...])
    edge = jnp.where(seq > 0, edge, 0.0)
    for r in range(8):
        shifted[r, r : r + TAPS, :] = edge

    forward(k_all, k_send, k_recv, 0)

    chunk = 64

    def filter_chunk(c, _):
        base = TAPS + c * chunk

        def eight(j, total):
            coeff = taps_t[pl.ds(pl.multiple_of(j * 8, 8), 8), :]
            rows = pl.ds(pl.multiple_of(base - j * 8, 8), chunk)
            for r in range(8):
                total = total + shifted[r, rows, :] * coeff[r : r + 1, :]
            return total

        total = lax.fori_loop(0, TAPS // 8, eight, jnp.zeros((chunk, WIDTH), jnp.float32))
        here = pl.ds(pl.multiple_of(c * chunk, chunk), chunk)
        hyena = (sq_ref[here, :].astype(jnp.float32) * total).astype(jnp.bfloat16)
        filtered[here, :] = res_ref[here, :].astype(jnp.float32) + hyena.astype(jnp.float32)
        return 0

    lax.fori_loop(0, ROWS // chunk, filter_chunk, 0)
    summed = filtered[...]
    own_square = jnp.sum(summed * summed, axis=1, keepdims=True)
    squares[mp] = jnp.broadcast_to(own_square, (ROWS, 128)).T[:8]
    for d in range(1, nm):
        copy = remote(
            squares.at[mp], squares.at[mp], sq_send.at[d], sq_recv.at[mp],
            at_mp(lax.rem(mp + d, nm)),
        )
        copy.start()
        sends.append(copy)
    for d in range(1, nm):
        source = lax.rem(mp + d, nm)
        remote(
            squares.at[source], squares.at[source], sq_send.at[d], sq_recv.at[source],
            at_mp(source),
        ).wait_recv()
    square = squares[0]
    for i in range(1, nm):
        square = square + squares[i]
    inverse = lax.rsqrt(square / (nm * WIDTH) + EPS)
    inverse = jnp.concatenate([inverse] * 16, axis=0).T
    inverse = jnp.concatenate([inverse] * (WIDTH // 128), axis=1)
    scaled = filtered[...] * inverse * gain_ref[...]
    v_all[mine] = scaled.T.astype(jnp.bfloat16)

    @pl.when(zh == 0)
    def _():
        across(v_all.at[mine], v_all, v_send, v_recv).start()

    spread(v_all.at[mine], v_all, v_send, v_recv, 0)
    normed_ref[...] = scaled.astype(jnp.bfloat16)

    @pl.when(zh == 1)
    def _():
        arrived(k_all, k_send, k_recv)
        spread(k_all.at[other], k_all, k_send, k_recv, 1)

    forward(v_all, v_send, v_recv, 0)

    @pl.when(zh == 1)
    def _():
        forward(k_all, k_send, k_recv, 1)
        arrived(v_all, v_send, v_recv)
        spread(v_all.at[other], v_all, v_send, v_recv, 1)
        forward(v_all, v_send, v_recv, 1)

    for d in range(1, ny):
        source = lax.rem(y + d, ny)
        remote(
            q_all.at[source], q_all.at[source], q_send.at[d], q_recv.at[source], at_y(source)
        ).wait_recv()
    for gather in gathers:
        finish(*gather, 0)

    @pl.when(zh == 1)
    def _():
        for gather in gathers:
            finish(*gather, 1)

    def tile(h, q_slot, slot, masked):
        lanes = slice(h * HD, (h + 1) * HD)
        score = lax.dot_general(
            k_all[slot, :, lanes], q_all[q_slot, :, lanes], (((1,), (1,)), ((), ())),
            preferred_element_type=jnp.float32,
        ) * SCALE2
        if masked:
            key = lax.broadcasted_iota(jnp.int32, (ROWS, ROWS), 0)
            query = lax.broadcasted_iota(jnp.int32, (ROWS, ROWS), 1)
            score = jnp.where(key <= query, score, LOW)
        before = m_ref[h]
        now = jnp.maximum(before, jnp.max(score, axis=0, keepdims=True))
        m_ref[h] = now
        weight = jnp.exp2(score - now)
        factor = jnp.exp2(before - now)
        l_ref[h] = l_ref[h] * factor + jnp.sum(weight, axis=0, keepdims=True)
        acc_ref[h] = acc_ref[h] * factor + jnp.dot(
            v_all[slot, lanes, :], weight.astype(jnp.bfloat16),
            preferred_element_type=jnp.float32,
        )

    def query_block(i, _):
        q_slot = lax.rem(y + 1 + i, ny)
        is_own = i == ny - 1
        m_ref[...] = jnp.full_like(m_ref, LOW)
        l_ref[...] = jnp.zeros_like(l_ref)
        acc_ref[...] = jnp.zeros_like(acc_ref)
        inside = jnp.where(q_slot > y, nx, jnp.where(is_own, x, 0))
        count = zh * nx + inside

        def step(slot, carry):
            for h in range(HEADS):
                tile(h, q_slot, slot, False)
            return carry

        lax.fori_loop(0, count, step, 0)

        @pl.when(is_own)
        def _():
            for h in range(HEADS):
                tile(h, q_slot, mine, True)

        logs = []
        for h in range(HEADS):
            amount = l_ref[h]
            amount = jnp.where(amount > 0.0, amount, 1.0)
            part[q_slot, :, h * HD : (h + 1) * HD] = (acc_ref[h] / amount).T.astype(jnp.bfloat16)
            logs.append(m_ref[h] + jnp.log2(amount))
        head = lax.broadcasted_iota(jnp.int32, (8, ROWS), 0)
        stat[q_slot] = jnp.where(head == 0, logs[0], logs[1])

        @pl.when(jnp.logical_not(is_own))
        def _():
            remote(
                part.at[q_slot], part_in.at[y], p_send.at[q_slot], p_recv.at[y], at_y(q_slot)
            ).start()
            remote(
                stat.at[q_slot], stat_in.at[y], s_send.at[q_slot], s_recv.at[y], at_y(q_slot)
            ).start()

        return 0

    lax.fori_loop(0, ny, query_block, 0)

    for d in range(1, ny):
        source = lax.rem(y + d, ny)
        last = remote(
            part.at[source], part_in.at[source], p_send.at[source], p_recv.at[source],
            at_y(source),
        )
        last.wait()
        last = remote(
            stat.at[source], stat_in.at[source], s_send.at[source], s_recv.at[source],
            at_y(source),
        )
        last.wait()

    stats = [stat[y]] + [stat_in[lax.rem(y + d, ny)] for d in range(1, ny)]
    top = functools.reduce(jnp.maximum, stats)
    raised = [jnp.exp2(s - top) for s in stats]
    norm = functools.reduce(jnp.add, raised)
    share = jnp.concatenate([e / norm for e in raised], axis=0)
    if ny < 16:
        share = jnp.concatenate([share, jnp.zeros((128 - 8 * ny, ROWS), jnp.float32)], axis=0)
    share = share.T
    for h in range(HEADS):
        lanes = slice(h * HD, (h + 1) * HD)
        total = share[:, h : h + 1] * part[y, :, lanes].astype(jnp.float32)
        for d in range(1, ny):
            piece = part_in[lax.rem(y + d, ny), :, lanes].astype(jnp.float32)
            total = total + share[:, d * 8 + h : d * 8 + h + 1] * piece
        out_ref[:, lanes] = total.astype(jnp.bfloat16)

    for copy in sends:
        copy.wait_send()
    for src, (table, send, recv) in zip((k_ref, v_all.at[mine]), gathers):
        spread(src, table, send, recv, 0, "wait_send")
        forward(table, send, recv, 0, "wait_send")

        @pl.when(zh == 0)
        def _():
            across(src, table, send, recv).wait_send()

        @pl.when(zh == 1)
        def _():
            spread(table.at[other], table, send, recv, 1, "wait_send")
            forward(table, send, recv, 1, "wait_send")


def build(mesh, sizes):
    nz, ny, nx, nm = sizes
    group = nz * nx

    def local(stream_q, stream_k, stream_v, taps, decay, residual, gain, queries, keys):
        block = jax.ShapeDtypeStruct((ROWS, WIDTH), jnp.bfloat16)
        bf, f32 = jnp.bfloat16, jnp.float32
        vmem = pltpu.VMEM
        dma = pltpu.SemaphoreType.DMA
        return pl.pallas_call(
            functools.partial(body, sizes),
            out_shape=(block, block),
            in_specs=[pl.BlockSpec(memory_space=pltpu.VMEM)] * 9,
            out_specs=(pl.BlockSpec(memory_space=pltpu.VMEM),) * 2,
            scratch_shapes=[
                vmem((TAPS, WIDTH), bf), vmem((TAPS, WIDTH), bf),
                vmem((8, TAPS + ROWS + 8, WIDTH), f32), vmem((TAPS, WIDTH), f32),
                vmem((ROWS, WIDTH), f32), vmem((nm, 8, ROWS), f32),
                vmem((ny, ROWS, WIDTH), bf), vmem((group, ROWS, WIDTH), bf),
                vmem((group, ROWS, WIDTH), bf), vmem((ny, ROWS, WIDTH), bf),
                vmem((ny, ROWS, WIDTH), bf), vmem((ny, 8, ROWS), f32), vmem((ny, 8, ROWS), f32),
                vmem((HEADS, 1, ROWS), f32), vmem((HEADS, 1, ROWS), f32),
                vmem((HEADS, HD, ROWS), f32),
                dma((2,)), dma((2,)), dma((nm,)), dma((nm,)), dma((ny,)), dma((ny,)),
                dma((9,)), dma((9,)), dma((9,)), dma((9,)),
                dma((ny,)), dma((ny,)), dma((ny,)), dma((ny,)),
            ],
            compiler_params=pltpu.CompilerParams(
                collective_id=0, has_side_effects=True, vmem_limit_bytes=60 * 1024 * 1024
            ),
        )(
            stream_q, stream_k, stream_v, taps, decay.reshape(1, WIDTH), residual,
            gain.reshape(1, WIDTH), queries, keys,
        )

    inner = Mesh(mesh.devices.reshape(sizes), AXES)
    rows = ("zh", "y", "x")
    array = P(rows, "mp")
    return jax.shard_map(
        local, mesh=inner,
        in_specs=(array, array, array, P("mp", None), P("mp"), array, P("mp"), array, array),
        out_specs=(array, array), check_vma=False,
    )


def solution(mesh):
    seq, nm = mesh.shape["seq"], mesh.shape["mp"]
    return build(mesh, (2, seq // 8, 4, nm))
```

```python
import functools
import math

import jax
import jax.numpy as jnp
from jax import lax
from jax.experimental import pallas as pl
from jax.experimental.pallas import tpu as pltpu
from jax.sharding import Mesh, PartitionSpec as P

HD = 128
ROWS = 256
WIDTH = 256
TAPS = 128
HEADS = WIDTH // HD
EPS = 1e-06
LOW = -1e30
SCALE2 = math.log2(math.e) / math.sqrt(HD)
MESH = pl.DeviceIdType.MESH
AXES = ("zh", "y", "x", "mp")


def body(
    sizes,
    sq_ref, sk_ref, sv_ref, taps_ref, decay_ref, res_ref, gain_ref, q_ref, k_ref,
    normed_ref, out_ref,
    halo_k, halo_v, shifted, taps_t, filtered, squares,
    q_all, k_all, v_all, part, part_in, stat, stat_in, m_ref, l_ref, acc_ref,
    halo_send, halo_recv, sq_send, sq_recv, q_send, q_recv,
    k_send, k_recv, v_send, v_recv, p_send, p_recv, s_send, s_recv,
):
    nz, ny, nx, nm = sizes
    zh, y, x, mp = (lax.axis_index(name) for name in AXES)
    seq = (zh * ny + y) * nx + x
    mine = zh * nx + x
    other = (1 - zh) * nx + x
    total_seq = nz * ny * nx

    def at_seq(s):
        return (s // (ny * nx), lax.rem(s // nx, ny), lax.rem(s, nx), mp)

    def at_y(p):
        return (zh, p, x, mp)

    def at_x(p):
        return (zh, y, p, mp)

    def at_mp(p):
        return (zh, y, x, p)

    partner = (1 - zh, y, x, mp)
    following = at_seq(lax.rem(seq + 1, total_seq))
    previous = at_seq(lax.rem(seq + total_seq - 1, total_seq))

    def remote(src, dst, send, recv, device):
        return pltpu.make_async_remote_copy(
            src_ref=src, dst_ref=dst, send_sem=send, recv_sem=recv,
            device_id=device, device_id_type=MESH,
        )

    barrier = pltpu.get_barrier_semaphore()
    greeted = [previous, partner]
    greeted += [at_y(lax.rem(y + d, ny)) for d in range(1, ny)]
    greeted += [at_x(lax.rem(x + d, nx)) for d in range(1, nx)]
    greeted += [at_mp(lax.rem(mp + d, nm)) for d in range(1, nm)]
    for device in greeted:
        pl.semaphore_signal(barrier, inc=1, device_id=device, device_id_type=MESH)
    pl.semaphore_wait(barrier, len(greeted))

    tail = pl.ds(ROWS - TAPS, TAPS)
    halos = [
        remote(sk_ref.at[tail], halo_k, halo_send.at[0], halo_recv.at[0], following),
        remote(sv_ref.at[tail], halo_v, halo_send.at[1], halo_recv.at[1], following),
    ]
    for copy in halos:
        copy.start()

    sends = []

    left, right = lax.rem(x + nx - 1, nx), lax.rem(x + 1, nx)
    halves = (pl.ds(0, ROWS // 2), pl.ds(ROWS // 2, ROWS // 2))

    def spread(src, table, send, recv, half, act="start"):
        slot = (zh if half == 0 else 1 - zh) * nx + x
        for kind, target in ((0, right), (1, left)):
            n = half * 4 + kind
            copy = remote(src, table.at[slot], send.at[n], recv.at[n], at_x(target))
            getattr(copy, act)()

    def forward(table, send, recv, half, act="start"):
        base = (zh if half == 0 else 1 - zh) * nx
        for kind, target, column in ((0, right, left), (1, left, right)):
            n = half * 4 + kind
            piece = table.at[base + column]
            if act == "start":
                remote(piece, piece, send.at[n], recv.at[n], at_x(target)).wait_recv()
            piece = piece.at[halves[kind]]
            copy = remote(piece, piece, send.at[n + 2], recv.at[n + 2], at_x(target))
            getattr(copy, act)()

    def finish(table, send, recv, half):
        far = (zh if half == 0 else 1 - zh) * nx + lax.rem(x + 2, nx)
        for kind in range(2):
            n = half * 4 + kind + 2
            piece = table.at[far].at[halves[kind]]
            remote(piece, piece, send.at[n], recv.at[n], at_x(left)).wait_recv()

    def across(src, table, send, recv):
        return remote(src, table.at[mine], send.at[8], recv.at[8], partner)

    def arrived(table, send, recv):
        remote(table.at[other], table.at[other], send.at[8], recv.at[8], partner).wait_recv()

    gathers = ((k_all, k_send, k_recv), (v_all, v_send, v_recv))

    @pl.when(zh == 0)
    def _():
        across(k_ref, k_all, k_send, k_recv).start()

    spread(k_ref, k_all, k_send, k_recv, 0)
    for d in range(1, ny):
        copy = remote(
            q_ref, q_all.at[y], q_send.at[d], q_recv.at[y], at_y(lax.rem(y + d, ny))
        )
        copy.start()
        sends.append(copy)
    q_all[y] = q_ref[...]
    k_all[mine] = k_ref[...]

    steps = lax.broadcasted_iota(jnp.int32, (TAPS, WIDTH), 0).astype(jnp.float32)
    taps_t[...] = taps_ref[...].T * jnp.exp(-decay_ref[...] * steps)

    def gate(a, b):
        return (a.astype(jnp.float32) * b.astype(jnp.float32)).astype(jnp.bfloat16).astype(jnp.float32)

    own_gated = gate(sk_ref[...], sv_ref[...])
    for r in range(8):
        shifted[r, TAPS + r : TAPS + r + ROWS, :] = own_gated
    for copy in halos:
        copy.wait()
    edge = gate(halo_k[...], halo_v[...])
    edge = jnp.where(seq > 0, edge, 0.0)
    for r in range(8):
        shifted[r, r : r + TAPS, :] = edge

    chunk = 64

    def filter_chunk(c, _):
        base = TAPS + c * chunk

        def eight(j, total):
            coeff = taps_t[pl.ds(pl.multiple_of(j * 8, 8), 8), :]
            rows = pl.ds(pl.multiple_of(base - j * 8, 8), chunk)
            for r in range(8):
                total = total + shifted[r, rows, :] * coeff[r : r + 1, :]
            return total

        total = lax.fori_loop(0, TAPS // 8, eight, jnp.zeros((chunk, WIDTH), jnp.float32))
        here = pl.ds(pl.multiple_of(c * chunk, chunk), chunk)
        hyena = (sq_ref[here, :].astype(jnp.float32) * total).astype(jnp.bfloat16)
        filtered[here, :] = res_ref[here, :].astype(jnp.float32) + hyena.astype(jnp.float32)
        return 0

    lax.fori_loop(0, ROWS // chunk, filter_chunk, 0)
    summed = filtered[...]
    own_square = jnp.sum(summed * summed, axis=1, keepdims=True)
    squares[mp] = jnp.broadcast_to(own_square, (ROWS, 128)).T[:8]
    for d in range(1, nm):
        copy = remote(
            squares.at[mp], squares.at[mp], sq_send.at[d], sq_recv.at[mp],
            at_mp(lax.rem(mp + d, nm)),
        )
        copy.start()
        sends.append(copy)
    for d in range(1, nm):
        source = lax.rem(mp + d, nm)
        remote(
            squares.at[source], squares.at[source], sq_send.at[d], sq_recv.at[source],
            at_mp(source),
        ).wait_recv()
    square = squares[0]
    for i in range(1, nm):
        square = square + squares[i]
    inverse = lax.rsqrt(square / (nm * WIDTH) + EPS)
    inverse = jnp.concatenate([inverse] * 16, axis=0).T
    inverse = jnp.concatenate([inverse] * (WIDTH // 128), axis=1)
    scaled = filtered[...] * inverse * gain_ref[...]
    v_all[mine] = scaled.T.astype(jnp.bfloat16)

    @pl.when(zh == 0)
    def _():
        across(v_all.at[mine], v_all, v_send, v_recv).start()

    spread(v_all.at[mine], v_all, v_send, v_recv, 0)
    normed_ref[...] = scaled.astype(jnp.bfloat16)
    forward(k_all, k_send, k_recv, 0)

    @pl.when(zh == 1)
    def _():
        arrived(k_all, k_send, k_recv)
        spread(k_all.at[other], k_all, k_send, k_recv, 1)

    forward(v_all, v_send, v_recv, 0)

    @pl.when(zh == 1)
    def _():
        forward(k_all, k_send, k_recv, 1)
        arrived(v_all, v_send, v_recv)
        spread(v_all.at[other], v_all, v_send, v_recv, 1)
        forward(v_all, v_send, v_recv, 1)

    for d in range(1, ny):
        source = lax.rem(y + d, ny)
        remote(
            q_all.at[source], q_all.at[source], q_send.at[d], q_recv.at[source], at_y(source)
        ).wait_recv()
    for gather in gathers:
        finish(*gather, 0)

    @pl.when(zh == 1)
    def _():
        for gather in gathers:
            finish(*gather, 1)

    def group(h, q_slot, base, masked):
        lanes = slice(h * HD, (h + 1) * HD)
        query = q_all[q_slot, :, lanes]
        scores = []
        for c in range(nx):
            score = lax.dot_general(
                k_all[base + c, :, lanes], query, (((1,), (1,)), ((), ())),
                preferred_element_type=jnp.float32,
            )
            if masked:
                key_pos = lax.broadcasted_iota(jnp.int32, (ROWS, ROWS), 0) + c * ROWS
                query_pos = lax.broadcasted_iota(jnp.int32, (ROWS, ROWS), 1) + x * ROWS
                score = jnp.where(key_pos <= query_pos, score, LOW)
            scores.append(score)
        before = m_ref[h]
        top = functools.reduce(jnp.maximum, scores)
        now = jnp.maximum(before, jnp.max(top, axis=0, keepdims=True) * SCALE2)
        m_ref[h] = now
        factor = jnp.exp2(before - now)
        weights = [jnp.exp2(score * SCALE2 - now) for score in scores]
        summed = functools.reduce(jnp.add, weights)
        l_ref[h] = l_ref[h] * factor + jnp.sum(summed, axis=0, keepdims=True)
        total = acc_ref[h] * factor
        for c in range(nx):
            total = total + jnp.dot(
                v_all[base + c, lanes, :], weights[c].astype(jnp.bfloat16),
                preferred_element_type=jnp.float32,
            )
        acc_ref[h] = total

    def query_block(i, _):
        q_slot = lax.rem(y + 1 + i, ny)
        is_own = i == ny - 1
        m_ref[...] = jnp.full_like(m_ref, LOW)
        l_ref[...] = jnp.zeros_like(l_ref)
        acc_ref[...] = jnp.zeros_like(acc_ref)
        count = zh + jnp.where(q_slot > y, 1, 0)

        def step(i, carry):
            for h in range(HEADS):
                group(h, q_slot, i * nx, False)
            return carry

        lax.fori_loop(0, count, step, 0)

        @pl.when(is_own)
        def _():
            for h in range(HEADS):
                group(h, q_slot, zh * nx, True)

        logs = []
        for h in range(HEADS):
            amount = l_ref[h]
            amount = jnp.where(amount > 0.0, amount, 1.0)
            part[q_slot, :, h * HD : (h + 1) * HD] = (acc_ref[h] / amount).T.astype(jnp.bfloat16)
            logs.append(m_ref[h] + jnp.log2(amount))
        head = lax.broadcasted_iota(jnp.int32, (8, ROWS), 0)
        stat[q_slot] = jnp.where(head == 0, logs[0], logs[1])

        @pl.when(jnp.logical_not(is_own))
        def _():
            remote(
                part.at[q_slot], part_in.at[y], p_send.at[q_slot], p_recv.at[y], at_y(q_slot)
            ).start()
            remote(
                stat.at[q_slot], stat_in.at[y], s_send.at[q_slot], s_recv.at[y], at_y(q_slot)
            ).start()

        return 0

    lax.fori_loop(0, ny, query_block, 0)

    for d in range(1, ny):
        source = lax.rem(y + d, ny)
        last = remote(
            part.at[source], part_in.at[source], p_send.at[source], p_recv.at[source],
            at_y(source),
        )
        last.wait()
        last = remote(
            stat.at[source], stat_in.at[source], s_send.at[source], s_recv.at[source],
            at_y(source),
        )
        last.wait()

    stats = [stat[y]] + [stat_in[lax.rem(y + d, ny)] for d in range(1, ny)]
    top = functools.reduce(jnp.maximum, stats)
    raised = [jnp.exp2(s - top) for s in stats]
    norm = functools.reduce(jnp.add, raised)
    share = jnp.concatenate([e / norm for e in raised], axis=0)
    if ny < 16:
        share = jnp.concatenate([share, jnp.zeros((128 - 8 * ny, ROWS), jnp.float32)], axis=0)
    share = share.T
    for h in range(HEADS):
        lanes = slice(h * HD, (h + 1) * HD)
        total = share[:, h : h + 1] * part[y, :, lanes].astype(jnp.float32)
        for d in range(1, ny):
            piece = part_in[lax.rem(y + d, ny), :, lanes].astype(jnp.float32)
            total = total + share[:, d * 8 + h : d * 8 + h + 1] * piece
        out_ref[:, lanes] = total.astype(jnp.bfloat16)

    for copy in sends:
        copy.wait_send()
    for src, (table, send, recv) in zip((k_ref, v_all.at[mine]), gathers):
        spread(src, table, send, recv, 0, "wait_send")
        forward(table, send, recv, 0, "wait_send")

        @pl.when(zh == 0)
        def _():
            across(src, table, send, recv).wait_send()

        @pl.when(zh == 1)
        def _():
            spread(table.at[other], table, send, recv, 1, "wait_send")
            forward(table, send, recv, 1, "wait_send")


def build(mesh, sizes):
    nz, ny, nx, nm = sizes
    group = nz * nx

    def local(stream_q, stream_k, stream_v, taps, decay, residual, gain, queries, keys):
        block = jax.ShapeDtypeStruct((ROWS, WIDTH), jnp.bfloat16)
        bf, f32 = jnp.bfloat16, jnp.float32
        vmem = pltpu.VMEM
        dma = pltpu.SemaphoreType.DMA
        return pl.pallas_call(
            functools.partial(body, sizes),
            out_shape=(block, block),
            in_specs=[pl.BlockSpec(memory_space=pltpu.VMEM)] * 9,
            out_specs=(pl.BlockSpec(memory_space=pltpu.VMEM),) * 2,
            scratch_shapes=[
                vmem((TAPS, WIDTH), bf), vmem((TAPS, WIDTH), bf),
                vmem((8, TAPS + ROWS + 8, WIDTH), f32), vmem((TAPS, WIDTH), f32),
                vmem((ROWS, WIDTH), f32), vmem((nm, 8, ROWS), f32),
                vmem((ny, ROWS, WIDTH), bf), vmem((group, ROWS, WIDTH), bf),
                vmem((group, ROWS, WIDTH), bf), vmem((ny, ROWS, WIDTH), bf),
                vmem((ny, ROWS, WIDTH), bf), vmem((ny, 8, ROWS), f32), vmem((ny, 8, ROWS), f32),
                vmem((HEADS, 1, ROWS), f32), vmem((HEADS, 1, ROWS), f32),
                vmem((HEADS, HD, ROWS), f32),
                dma((2,)), dma((2,)), dma((nm,)), dma((nm,)), dma((ny,)), dma((ny,)),
                dma((9,)), dma((9,)), dma((9,)), dma((9,)),
                dma((ny,)), dma((ny,)), dma((ny,)), dma((ny,)),
            ],
            compiler_params=pltpu.CompilerParams(
                collective_id=0, has_side_effects=True, vmem_limit_bytes=60 * 1024 * 1024
            ),
        )(
            stream_q, stream_k, stream_v, taps, decay.reshape(1, WIDTH), residual,
            gain.reshape(1, WIDTH), queries, keys,
        )

    inner = Mesh(mesh.devices.reshape(sizes), AXES)
    rows = ("zh", "y", "x")
    array = P(rows, "mp")
    return jax.shard_map(
        local, mesh=inner,
        in_specs=(array, array, array, P("mp", None), P("mp"), array, P("mp"), array, array),
        out_specs=(array, array), check_vma=False,
    )


def solution(mesh):
    seq, nm = mesh.shape["seq"], mesh.shape["mp"]
    return build(mesh, (2, seq // 8, 4, nm))
```

```python
import functools
import math

import jax
import jax.numpy as jnp
from jax import lax
from jax.experimental import pallas as pl
from jax.experimental.pallas import tpu as pltpu
from jax.sharding import Mesh, PartitionSpec as P

HD = 128
ROWS = 256
WIDTH = 256
TAPS = 128
HEADS = WIDTH // HD
EPS = 1e-06
LOW = -1e30
SCALE2 = math.log2(math.e) / math.sqrt(HD)
MESH = pl.DeviceIdType.MESH
AXES = ("zh", "y", "x", "mp")


def body(
    sizes,
    sq_ref, sk_ref, sv_ref, taps_ref, decay_ref, res_ref, gain_ref, q_ref, k_ref,
    normed_ref, out_ref,
    halo_k, halo_v, shifted, taps_t, filtered, squares,
    q_all, k_all, v_all, part, part_in, stat, stat_in, m_ref, l_ref, acc_ref,
    halo_send, halo_recv, sq_send, sq_recv, q_send, q_recv,
    k_send, k_recv, v_send, v_recv, p_send, p_recv, s_send, s_recv,
):
    nz, ny, nx, nm = sizes
    zh, y, x, mp = (lax.axis_index(name) for name in AXES)
    seq = (zh * ny + y) * nx + x
    mine = zh * nx + x
    other = (1 - zh) * nx + x
    total_seq = nz * ny * nx

    def at_seq(s):
        return (s // (ny * nx), lax.rem(s // nx, ny), lax.rem(s, nx), mp)

    def at_y(p):
        return (zh, p, x, mp)

    def at_x(p):
        return (zh, y, p, mp)

    def at_mp(p):
        return (zh, y, x, p)

    partner = (1 - zh, y, x, mp)
    following = at_seq(lax.rem(seq + 1, total_seq))
    previous = at_seq(lax.rem(seq + total_seq - 1, total_seq))

    def remote(src, dst, send, recv, device):
        return pltpu.make_async_remote_copy(
            src_ref=src, dst_ref=dst, send_sem=send, recv_sem=recv,
            device_id=device, device_id_type=MESH,
        )

    barrier = pltpu.get_barrier_semaphore()
    greeted = [previous, partner]
    greeted += [at_y(lax.rem(y + d, ny)) for d in range(1, ny)]
    greeted += [at_x(lax.rem(x + d, nx)) for d in range(1, nx)]
    greeted += [at_mp(lax.rem(mp + d, nm)) for d in range(1, nm)]
    for device in greeted:
        pl.semaphore_signal(barrier, inc=1, device_id=device, device_id_type=MESH)
    pl.semaphore_wait(barrier, len(greeted))

    tail = pl.ds(ROWS - TAPS, TAPS)
    halos = [
        remote(sk_ref.at[tail], halo_k, halo_send.at[0], halo_recv.at[0], following),
        remote(sv_ref.at[tail], halo_v, halo_send.at[1], halo_recv.at[1], following),
    ]
    for copy in halos:
        copy.start()

    sends = []

    left, right = lax.rem(x + nx - 1, nx), lax.rem(x + 1, nx)
    halves = (pl.ds(0, ROWS // 2), pl.ds(ROWS // 2, ROWS // 2))

    def spread(src, table, send, recv, half, act="start"):
        slot = (zh if half == 0 else 1 - zh) * nx + x
        for kind, target in ((0, right), (1, left)):
            n = half * 4 + kind
            copy = remote(src, table.at[slot], send.at[n], recv.at[n], at_x(target))
            getattr(copy, act)()

    def forward(table, send, recv, half, act="start"):
        base = (zh if half == 0 else 1 - zh) * nx
        for kind, target, column in ((0, right, left), (1, left, right)):
            n = half * 4 + kind
            piece = table.at[base + column]
            if act == "start":
                remote(piece, piece, send.at[n], recv.at[n], at_x(target)).wait_recv()
            piece = piece.at[halves[kind]]
            copy = remote(piece, piece, send.at[n + 2], recv.at[n + 2], at_x(target))
            getattr(copy, act)()

    def finish(table, send, recv, half):
        far = (zh if half == 0 else 1 - zh) * nx + lax.rem(x + 2, nx)
        for kind in range(2):
            n = half * 4 + kind + 2
            piece = table.at[far].at[halves[kind]]
            remote(piece, piece, send.at[n], recv.at[n], at_x(left)).wait_recv()

    def across(src, table, send, recv):
        return remote(src, table.at[mine], send.at[8], recv.at[8], partner)

    def arrived(table, send, recv):
        remote(table.at[other], table.at[other], send.at[8], recv.at[8], partner).wait_recv()

    gathers = ((k_all, k_send, k_recv), (v_all, v_send, v_recv))

    q_all[y] = q_ref[...]
    k_all[mine] = k_ref[...]

    steps = lax.broadcasted_iota(jnp.int32, (TAPS, WIDTH), 0).astype(jnp.float32)
    taps_t[...] = taps_ref[...].T * jnp.exp(-decay_ref[...] * steps)

    def gate(a, b):
        return (a.astype(jnp.float32) * b.astype(jnp.float32)).astype(jnp.bfloat16).astype(jnp.float32)

    own_gated = gate(sk_ref[...], sv_ref[...])
    for r in range(8):
        shifted[r, TAPS + r : TAPS + r + ROWS, :] = own_gated
    for copy in halos:
        copy.wait()
    @pl.when(zh == 0)
    def _():
        across(k_ref, k_all, k_send, k_recv).start()

    spread(k_ref, k_all, k_send, k_recv, 0)
    for d in range(1, ny):
        copy = remote(
            q_ref, q_all.at[y], q_send.at[d], q_recv.at[y], at_y(lax.rem(y + d, ny))
        )
        copy.start()
        sends.append(copy)
    edge = gate(halo_k[...], halo_v[...])
    edge = jnp.where(seq > 0, edge, 0.0)
    for r in range(8):
        shifted[r, r : r + TAPS, :] = edge

    chunk = 64

    def filter_chunk(c, _):
        base = TAPS + c * chunk

        def eight(j, total):
            coeff = taps_t[pl.ds(pl.multiple_of(j * 8, 8), 8), :]
            rows = pl.ds(pl.multiple_of(base - j * 8, 8), chunk)
            for r in range(8):
                total = total + shifted[r, rows, :] * coeff[r : r + 1, :]
            return total

        total = lax.fori_loop(0, TAPS // 8, eight, jnp.zeros((chunk, WIDTH), jnp.float32))
        here = pl.ds(pl.multiple_of(c * chunk, chunk), chunk)
        hyena = (sq_ref[here, :].astype(jnp.float32) * total).astype(jnp.bfloat16)
        filtered[here, :] = res_ref[here, :].astype(jnp.float32) + hyena.astype(jnp.float32)
        return 0

    lax.fori_loop(0, ROWS // chunk, filter_chunk, 0)
    summed = filtered[...]
    own_square = jnp.sum(summed * summed, axis=1, keepdims=True)
    squares[mp] = jnp.broadcast_to(own_square, (ROWS, 128)).T[:8]
    for d in range(1, nm):
        copy = remote(
            squares.at[mp], squares.at[mp], sq_send.at[d], sq_recv.at[mp],
            at_mp(lax.rem(mp + d, nm)),
        )
        copy.start()
        sends.append(copy)
    for d in range(1, nm):
        source = lax.rem(mp + d, nm)
        remote(
            squares.at[source], squares.at[source], sq_send.at[d], sq_recv.at[source],
            at_mp(source),
        ).wait_recv()
    square = squares[0]
    for i in range(1, nm):
        square = square + squares[i]
    inverse = lax.rsqrt(square / (nm * WIDTH) + EPS)
    inverse = jnp.concatenate([inverse] * 16, axis=0).T
    inverse = jnp.concatenate([inverse] * (WIDTH // 128), axis=1)
    scaled = filtered[...] * inverse * gain_ref[...]
    v_all[mine] = scaled.T.astype(jnp.bfloat16)

    @pl.when(zh == 0)
    def _():
        across(v_all.at[mine], v_all, v_send, v_recv).start()

    spread(v_all.at[mine], v_all, v_send, v_recv, 0)
    normed_ref[...] = scaled.astype(jnp.bfloat16)
    forward(k_all, k_send, k_recv, 0)

    @pl.when(zh == 1)
    def _():
        arrived(k_all, k_send, k_recv)
        spread(k_all.at[other], k_all, k_send, k_recv, 1)

    forward(v_all, v_send, v_recv, 0)

    @pl.when(zh == 1)
    def _():
        forward(k_all, k_send, k_recv, 1)
        arrived(v_all, v_send, v_recv)
        spread(v_all.at[other], v_all, v_send, v_recv, 1)
        forward(v_all, v_send, v_recv, 1)

    for d in range(1, ny):
        source = lax.rem(y + d, ny)
        remote(
            q_all.at[source], q_all.at[source], q_send.at[d], q_recv.at[source], at_y(source)
        ).wait_recv()
    for gather in gathers:
        finish(*gather, 0)

    @pl.when(zh == 1)
    def _():
        for gather in gathers:
            finish(*gather, 1)

    def group(h, q_slot, base, masked):
        lanes = slice(h * HD, (h + 1) * HD)
        query = q_all[q_slot, :, lanes]
        scores = []
        for c in range(nx):
            score = lax.dot_general(
                k_all[base + c, :, lanes], query, (((1,), (1,)), ((), ())),
                preferred_element_type=jnp.float32,
            )
            if masked:
                key_pos = lax.broadcasted_iota(jnp.int32, (ROWS, ROWS), 0) + c * ROWS
                query_pos = lax.broadcasted_iota(jnp.int32, (ROWS, ROWS), 1) + x * ROWS
                score = jnp.where(key_pos <= query_pos, score, LOW)
            scores.append(score)
        before = m_ref[h]
        top = functools.reduce(jnp.maximum, scores)
        now = jnp.maximum(before, jnp.max(top, axis=0, keepdims=True) * SCALE2)
        m_ref[h] = now
        factor = jnp.exp2(before - now)
        weights = [jnp.exp2(score * SCALE2 - now) for score in scores]
        summed = functools.reduce(jnp.add, weights)
        l_ref[h] = l_ref[h] * factor + jnp.sum(summed, axis=0, keepdims=True)
        total = acc_ref[h] * factor
        for c in range(nx):
            total = total + jnp.dot(
                v_all[base + c, lanes, :], weights[c].astype(jnp.bfloat16),
                preferred_element_type=jnp.float32,
            )
        acc_ref[h] = total

    def query_block(i, _):
        q_slot = lax.rem(y + 1 + i, ny)
        is_own = i == ny - 1
        m_ref[...] = jnp.full_like(m_ref, LOW)
        l_ref[...] = jnp.zeros_like(l_ref)
        acc_ref[...] = jnp.zeros_like(acc_ref)
        count = zh + jnp.where(q_slot > y, 1, 0)

        def step(i, carry):
            for h in range(HEADS):
                group(h, q_slot, i * nx, False)
            return carry

        lax.fori_loop(0, count, step, 0)

        @pl.when(is_own)
        def _():
            for h in range(HEADS):
                group(h, q_slot, zh * nx, True)

        logs = []
        for h in range(HEADS):
            amount = l_ref[h]
            amount = jnp.where(amount > 0.0, amount, 1.0)
            part[q_slot, :, h * HD : (h + 1) * HD] = (acc_ref[h] / amount).T.astype(jnp.bfloat16)
            logs.append(m_ref[h] + jnp.log2(amount))
        head = lax.broadcasted_iota(jnp.int32, (8, ROWS), 0)
        stat[q_slot] = jnp.where(head == 0, logs[0], logs[1])

        @pl.when(jnp.logical_not(is_own))
        def _():
            remote(
                part.at[q_slot], part_in.at[y], p_send.at[q_slot], p_recv.at[y], at_y(q_slot)
            ).start()
            remote(
                stat.at[q_slot], stat_in.at[y], s_send.at[q_slot], s_recv.at[y], at_y(q_slot)
            ).start()

        return 0

    lax.fori_loop(0, ny, query_block, 0)

    for d in range(1, ny):
        source = lax.rem(y + d, ny)
        last = remote(
            part.at[source], part_in.at[source], p_send.at[source], p_recv.at[source],
            at_y(source),
        )
        last.wait()
        last = remote(
            stat.at[source], stat_in.at[source], s_send.at[source], s_recv.at[source],
            at_y(source),
        )
        last.wait()

    stats = [stat[y]] + [stat_in[lax.rem(y + d, ny)] for d in range(1, ny)]
    top = functools.reduce(jnp.maximum, stats)
    raised = [jnp.exp2(s - top) for s in stats]
    norm = functools.reduce(jnp.add, raised)
    share = jnp.concatenate([e / norm for e in raised], axis=0)
    if ny < 16:
        share = jnp.concatenate([share, jnp.zeros((128 - 8 * ny, ROWS), jnp.float32)], axis=0)
    share = share.T
    for h in range(HEADS):
        lanes = slice(h * HD, (h + 1) * HD)
        total = share[:, h : h + 1] * part[y, :, lanes].astype(jnp.float32)
        for d in range(1, ny):
            piece = part_in[lax.rem(y + d, ny), :, lanes].astype(jnp.float32)
            total = total + share[:, d * 8 + h : d * 8 + h + 1] * piece
        out_ref[:, lanes] = total.astype(jnp.bfloat16)

    for copy in sends:
        copy.wait_send()
    for src, (table, send, recv) in zip((k_ref, v_all.at[mine]), gathers):
        spread(src, table, send, recv, 0, "wait_send")
        forward(table, send, recv, 0, "wait_send")

        @pl.when(zh == 0)
        def _():
            across(src, table, send, recv).wait_send()

        @pl.when(zh == 1)
        def _():
            spread(table.at[other], table, send, recv, 1, "wait_send")
            forward(table, send, recv, 1, "wait_send")


def build(mesh, sizes):
    nz, ny, nx, nm = sizes
    group = nz * nx

    def local(stream_q, stream_k, stream_v, taps, decay, residual, gain, queries, keys):
        block = jax.ShapeDtypeStruct((ROWS, WIDTH), jnp.bfloat16)
        bf, f32 = jnp.bfloat16, jnp.float32
        vmem = pltpu.VMEM
        dma = pltpu.SemaphoreType.DMA
        return pl.pallas_call(
            functools.partial(body, sizes),
            out_shape=(block, block),
            in_specs=[pl.BlockSpec(memory_space=pltpu.VMEM)] * 9,
            out_specs=(pl.BlockSpec(memory_space=pltpu.VMEM),) * 2,
            scratch_shapes=[
                vmem((TAPS, WIDTH), bf), vmem((TAPS, WIDTH), bf),
                vmem((8, TAPS + ROWS + 8, WIDTH), f32), vmem((TAPS, WIDTH), f32),
                vmem((ROWS, WIDTH), f32), vmem((nm, 8, ROWS), f32),
                vmem((ny, ROWS, WIDTH), bf), vmem((group, ROWS, WIDTH), bf),
                vmem((group, ROWS, WIDTH), bf), vmem((ny, ROWS, WIDTH), bf),
                vmem((ny, ROWS, WIDTH), bf), vmem((ny, 8, ROWS), f32), vmem((ny, 8, ROWS), f32),
                vmem((HEADS, 1, ROWS), f32), vmem((HEADS, 1, ROWS), f32),
                vmem((HEADS, HD, ROWS), f32),
                dma((2,)), dma((2,)), dma((nm,)), dma((nm,)), dma((ny,)), dma((ny,)),
                dma((9,)), dma((9,)), dma((9,)), dma((9,)),
                dma((ny,)), dma((ny,)), dma((ny,)), dma((ny,)),
            ],
            compiler_params=pltpu.CompilerParams(
                collective_id=0, has_side_effects=True, vmem_limit_bytes=60 * 1024 * 1024
            ),
        )(
            stream_q, stream_k, stream_v, taps, decay.reshape(1, WIDTH), residual,
            gain.reshape(1, WIDTH), queries, keys,
        )

    inner = Mesh(mesh.devices.reshape(sizes), AXES)
    rows = ("zh", "y", "x")
    array = P(rows, "mp")
    return jax.shard_map(
        local, mesh=inner,
        in_specs=(array, array, array, P("mp", None), P("mp"), array, P("mp"), array, array),
        out_specs=(array, array), check_vma=False,
    )


def solution(mesh):
    seq, nm = mesh.shape["seq"], mesh.shape["mp"]
    return build(mesh, (2, seq // 8, 4, nm))
```

```python
import functools
import math

import jax
import jax.numpy as jnp
from jax import lax
from jax.experimental import pallas as pl
from jax.experimental.pallas import tpu as pltpu
from jax.sharding import Mesh, PartitionSpec as P

HD = 128
ROWS = 256
WIDTH = 256
TAPS = 128
HEADS = WIDTH // HD
EPS = 1e-06
LOW = -1e30
SCALE2 = math.log2(math.e) / math.sqrt(HD)
MESH = pl.DeviceIdType.MESH
AXES = ("zh", "y", "x", "mp")


def body(
    sizes,
    sq_ref, sk_ref, sv_ref, taps_ref, decay_ref, res_ref, gain_ref, q_ref, k_ref,
    normed_ref, out_ref,
    halo_k, halo_v, shifted, taps_t, filtered, squares,
    q_all, k_all, v_all, part, part_in, stat, stat_in, m_ref, l_ref, acc_ref,
    halo_send, halo_recv, sq_send, sq_recv, q_send, q_recv,
    k_send, k_recv, v_send, v_recv, p_send, p_recv, s_send, s_recv,
):
    nz, ny, nx, nm = sizes
    zh, y, x, mp = (lax.axis_index(name) for name in AXES)
    seq = (zh * ny + y) * nx + x
    mine = zh * nx + x
    other = (1 - zh) * nx + x
    total_seq = nz * ny * nx

    def at_seq(s):
        return (s // (ny * nx), lax.rem(s // nx, ny), lax.rem(s, nx), mp)

    def at_y(p):
        return (zh, p, x, mp)

    def at_x(p):
        return (zh, y, p, mp)

    def at_mp(p):
        return (zh, y, x, p)

    partner = (1 - zh, y, x, mp)
    following = at_seq(lax.rem(seq + 1, total_seq))
    previous = at_seq(lax.rem(seq + total_seq - 1, total_seq))

    def remote(src, dst, send, recv, device):
        return pltpu.make_async_remote_copy(
            src_ref=src, dst_ref=dst, send_sem=send, recv_sem=recv,
            device_id=device, device_id_type=MESH,
        )

    barrier = pltpu.get_barrier_semaphore()
    greeted = [previous, partner]
    greeted += [at_y(lax.rem(y + d, ny)) for d in range(1, ny)]
    greeted += [at_x(lax.rem(x + d, nx)) for d in range(1, nx)]
    greeted += [at_mp(lax.rem(mp + d, nm)) for d in range(1, nm)]
    for device in greeted:
        pl.semaphore_signal(barrier, inc=1, device_id=device, device_id_type=MESH)
    pl.semaphore_wait(barrier, len(greeted))

    tail = pl.ds(ROWS - TAPS, TAPS)
    halos = [
        remote(sk_ref.at[tail], halo_k, halo_send.at[0], halo_recv.at[0], following),
        remote(sv_ref.at[tail], halo_v, halo_send.at[1], halo_recv.at[1], following),
    ]
    for copy in halos:
        copy.start()

    sends = []

    left, right = lax.rem(x + nx - 1, nx), lax.rem(x + 1, nx)
    halves = (pl.ds(0, ROWS // 2), pl.ds(ROWS // 2, ROWS // 2))

    def spread(src, table, send, recv, half, act="start"):
        slot = (zh if half == 0 else 1 - zh) * nx + x
        for kind, target in ((0, right), (1, left)):
            n = half * 4 + kind
            copy = remote(src, table.at[slot], send.at[n], recv.at[n], at_x(target))
            getattr(copy, act)()

    def forward(table, send, recv, half, act="start"):
        base = (zh if half == 0 else 1 - zh) * nx
        for kind, target, column in ((0, right, left), (1, left, right)):
            n = half * 4 + kind
            piece = table.at[base + column]
            if act == "start":
                remote(piece, piece, send.at[n], recv.at[n], at_x(target)).wait_recv()
            piece = piece.at[halves[kind]]
            copy = remote(piece, piece, send.at[n + 2], recv.at[n + 2], at_x(target))
            getattr(copy, act)()

    def finish(table, send, recv, half):
        far = (zh if half == 0 else 1 - zh) * nx + lax.rem(x + 2, nx)
        for kind in range(2):
            n = half * 4 + kind + 2
            piece = table.at[far].at[halves[kind]]
            remote(piece, piece, send.at[n], recv.at[n], at_x(left)).wait_recv()

    def across(src, table, send, recv):
        return remote(src, table.at[mine], send.at[8], recv.at[8], partner)

    def arrived(table, send, recv):
        remote(table.at[other], table.at[other], send.at[8], recv.at[8], partner).wait_recv()

    gathers = ((k_all, k_send, k_recv), (v_all, v_send, v_recv))

    @pl.when(zh == 0)
    def _():
        across(k_ref, k_all, k_send, k_recv).start()

    spread(k_ref, k_all, k_send, k_recv, 0)
    for d in range(1, ny):
        copy = remote(
            q_ref, q_all.at[y], q_send.at[d], q_recv.at[y], at_y(lax.rem(y + d, ny))
        )
        copy.start()
        sends.append(copy)
    q_all[y] = q_ref[...]
    k_all[mine] = k_ref[...]

    steps = lax.broadcasted_iota(jnp.int32, (TAPS, WIDTH), 0).astype(jnp.float32)
    taps_t[...] = taps_ref[...].T * jnp.exp(-decay_ref[...] * steps)

    def gate(a, b):
        return (a.astype(jnp.float32) * b.astype(jnp.float32)).astype(jnp.bfloat16).astype(jnp.float32)

    own_gated = gate(sk_ref[...], sv_ref[...])
    for r in range(8):
        shifted[r, TAPS + r : TAPS + r + ROWS, :] = own_gated
    for copy in halos:
        copy.wait()
    edge = gate(halo_k[...], halo_v[...])
    edge = jnp.where(seq > 0, edge, 0.0)
    for r in range(8):
        shifted[r, r : r + TAPS, :] = edge

    chunk = 64

    def filter_chunk(c, _):
        base = TAPS + c * chunk

        def eight(j, total):
            coeff = taps_t[pl.ds(pl.multiple_of(j * 8, 8), 8), :]
            rows = pl.ds(pl.multiple_of(base - j * 8, 8), chunk)
            for r in range(8):
                total = total + shifted[r, rows, :] * coeff[r : r + 1, :]
            return total

        total = lax.fori_loop(0, TAPS // 8, eight, jnp.zeros((chunk, WIDTH), jnp.float32))
        here = pl.ds(pl.multiple_of(c * chunk, chunk), chunk)
        hyena = (sq_ref[here, :].astype(jnp.float32) * total).astype(jnp.bfloat16)
        filtered[here, :] = res_ref[here, :].astype(jnp.float32) + hyena.astype(jnp.float32)
        return 0

    lax.fori_loop(0, ROWS // chunk, filter_chunk, 0)
    summed = filtered[...]
    own_square = jnp.sum(summed * summed, axis=1, keepdims=True)
    squares[mp] = jnp.broadcast_to(own_square, (ROWS, 128)).T[:8]
    for d in range(1, nm):
        copy = remote(
            squares.at[mp], squares.at[mp], sq_send.at[d], sq_recv.at[mp],
            at_mp(lax.rem(mp + d, nm)),
        )
        copy.start()
        sends.append(copy)
    for d in range(1, nm):
        source = lax.rem(mp + d, nm)
        remote(
            squares.at[source], squares.at[source], sq_send.at[d], sq_recv.at[source],
            at_mp(source),
        ).wait_recv()
    square = squares[0]
    for i in range(1, nm):
        square = square + squares[i]
    inverse = lax.rsqrt(square / (nm * WIDTH) + EPS)
    inverse = jnp.concatenate([inverse] * 16, axis=0).T
    inverse = jnp.concatenate([inverse] * (WIDTH // 128), axis=1)
    scaled = filtered[...] * inverse * gain_ref[...]
    v_all[mine] = scaled.T.astype(jnp.bfloat16)

    @pl.when(zh == 0)
    def _():
        across(v_all.at[mine], v_all, v_send, v_recv).start()

    spread(v_all.at[mine], v_all, v_send, v_recv, 0)
    normed_ref[...] = scaled.astype(jnp.bfloat16)
    forward(k_all, k_send, k_recv, 0)

    @pl.when(zh == 1)
    def _():
        arrived(k_all, k_send, k_recv)
        spread(k_all.at[other], k_all, k_send, k_recv, 1)

    forward(v_all, v_send, v_recv, 0)

    @pl.when(zh == 1)
    def _():
        forward(k_all, k_send, k_recv, 1)
        arrived(v_all, v_send, v_recv)
        spread(v_all.at[other], v_all, v_send, v_recv, 1)
        forward(v_all, v_send, v_recv, 1)

    for d in range(1, ny):
        source = lax.rem(y + d, ny)
        remote(
            q_all.at[source], q_all.at[source], q_send.at[d], q_recv.at[source], at_y(source)
        ).wait_recv()
    for gather in gathers:
        finish(*gather, 0)

    @pl.when(zh == 1)
    def _():
        for gather in gathers:
            finish(*gather, 1)

    def group(h, q_slot, base, masked):
        lanes = slice(h * HD, (h + 1) * HD)
        query = q_all[q_slot, :, lanes]
        scores = []
        for c in range(nx):
            score = lax.dot_general(
                k_all[base + c, :, lanes], query, (((1,), (1,)), ((), ())),
                preferred_element_type=jnp.float32,
            )
            if masked:
                key_pos = lax.broadcasted_iota(jnp.int32, (ROWS, ROWS), 0) + c * ROWS
                query_pos = lax.broadcasted_iota(jnp.int32, (ROWS, ROWS), 1) + x * ROWS
                score = jnp.where(key_pos <= query_pos, score, LOW)
            scores.append(score)
        before = m_ref[h]
        top = functools.reduce(jnp.maximum, scores)
        now = jnp.maximum(before, jnp.max(top, axis=0, keepdims=True) * SCALE2)
        m_ref[h] = now
        factor = jnp.exp2(before - now)
        weights = [jnp.exp2(score * SCALE2 - now) for score in scores]
        summed = functools.reduce(jnp.add, weights)
        l_ref[h] = l_ref[h] * factor + jnp.sum(summed, axis=0, keepdims=True)
        total = acc_ref[h] * factor
        for c in range(nx):
            total = total + jnp.dot(
                v_all[base + c, lanes, :], weights[c].astype(jnp.bfloat16),
                preferred_element_type=jnp.float32,
            )
        acc_ref[h] = total

    def query_block(i, _):
        away = (i + 1) // 2
        away = jnp.where(lax.rem(i, 2) == 1, ny // 2 - away, ny // 2 + away)
        q_slot = lax.rem(y + away, ny)
        is_own = i == ny - 1
        m_ref[...] = jnp.full_like(m_ref, LOW)
        l_ref[...] = jnp.zeros_like(l_ref)
        acc_ref[...] = jnp.zeros_like(acc_ref)
        count = zh + jnp.where(q_slot > y, 1, 0)

        def step(i, carry):
            for h in range(HEADS):
                group(h, q_slot, i * nx, False)
            return carry

        lax.fori_loop(0, count, step, 0)

        @pl.when(is_own)
        def _():
            for h in range(HEADS):
                group(h, q_slot, zh * nx, True)

        logs = []
        for h in range(HEADS):
            amount = l_ref[h]
            amount = jnp.where(amount > 0.0, amount, 1.0)
            part[q_slot, :, h * HD : (h + 1) * HD] = (acc_ref[h] / amount).T.astype(jnp.bfloat16)
            logs.append(m_ref[h] + jnp.log2(amount))
        head = lax.broadcasted_iota(jnp.int32, (8, ROWS), 0)
        stat[q_slot] = jnp.where(head == 0, logs[0], logs[1])

        @pl.when(jnp.logical_not(is_own))
        def _():
            remote(
                part.at[q_slot], part_in.at[y], p_send.at[q_slot], p_recv.at[y], at_y(q_slot)
            ).start()
            remote(
                stat.at[q_slot], stat_in.at[y], s_send.at[q_slot], s_recv.at[y], at_y(q_slot)
            ).start()

        return 0

    lax.fori_loop(0, ny, query_block, 0)

    for d in range(1, ny):
        source = lax.rem(y + d, ny)
        last = remote(
            part.at[source], part_in.at[source], p_send.at[source], p_recv.at[source],
            at_y(source),
        )
        last.wait()
        last = remote(
            stat.at[source], stat_in.at[source], s_send.at[source], s_recv.at[source],
            at_y(source),
        )
        last.wait()

    stats = [stat[y]] + [stat_in[lax.rem(y + d, ny)] for d in range(1, ny)]
    top = functools.reduce(jnp.maximum, stats)
    raised = [jnp.exp2(s - top) for s in stats]
    norm = functools.reduce(jnp.add, raised)
    share = jnp.concatenate([e / norm for e in raised], axis=0)
    if ny < 16:
        share = jnp.concatenate([share, jnp.zeros((128 - 8 * ny, ROWS), jnp.float32)], axis=0)
    share = share.T
    for h in range(HEADS):
        lanes = slice(h * HD, (h + 1) * HD)
        total = share[:, h : h + 1] * part[y, :, lanes].astype(jnp.float32)
        for d in range(1, ny):
            piece = part_in[lax.rem(y + d, ny), :, lanes].astype(jnp.float32)
            total = total + share[:, d * 8 + h : d * 8 + h + 1] * piece
        out_ref[:, lanes] = total.astype(jnp.bfloat16)

    for copy in sends:
        copy.wait_send()
    for src, (table, send, recv) in zip((k_ref, v_all.at[mine]), gathers):
        spread(src, table, send, recv, 0, "wait_send")
        forward(table, send, recv, 0, "wait_send")

        @pl.when(zh == 0)
        def _():
            across(src, table, send, recv).wait_send()

        @pl.when(zh == 1)
        def _():
            spread(table.at[other], table, send, recv, 1, "wait_send")
            forward(table, send, recv, 1, "wait_send")


def build(mesh, sizes):
    nz, ny, nx, nm = sizes
    group = nz * nx

    def local(stream_q, stream_k, stream_v, taps, decay, residual, gain, queries, keys):
        block = jax.ShapeDtypeStruct((ROWS, WIDTH), jnp.bfloat16)
        bf, f32 = jnp.bfloat16, jnp.float32
        vmem = pltpu.VMEM
        dma = pltpu.SemaphoreType.DMA
        return pl.pallas_call(
            functools.partial(body, sizes),
            out_shape=(block, block),
            in_specs=[pl.BlockSpec(memory_space=pltpu.VMEM)] * 9,
            out_specs=(pl.BlockSpec(memory_space=pltpu.VMEM),) * 2,
            scratch_shapes=[
                vmem((TAPS, WIDTH), bf), vmem((TAPS, WIDTH), bf),
                vmem((8, TAPS + ROWS + 8, WIDTH), f32), vmem((TAPS, WIDTH), f32),
                vmem((ROWS, WIDTH), f32), vmem((nm, 8, ROWS), f32),
                vmem((ny, ROWS, WIDTH), bf), vmem((group, ROWS, WIDTH), bf),
                vmem((group, ROWS, WIDTH), bf), vmem((ny, ROWS, WIDTH), bf),
                vmem((ny, ROWS, WIDTH), bf), vmem((ny, 8, ROWS), f32), vmem((ny, 8, ROWS), f32),
                vmem((HEADS, 1, ROWS), f32), vmem((HEADS, 1, ROWS), f32),
                vmem((HEADS, HD, ROWS), f32),
                dma((2,)), dma((2,)), dma((nm,)), dma((nm,)), dma((ny,)), dma((ny,)),
                dma((9,)), dma((9,)), dma((9,)), dma((9,)),
                dma((ny,)), dma((ny,)), dma((ny,)), dma((ny,)),
            ],
            compiler_params=pltpu.CompilerParams(
                collective_id=0, has_side_effects=True, vmem_limit_bytes=60 * 1024 * 1024
            ),
        )(
            stream_q, stream_k, stream_v, taps, decay.reshape(1, WIDTH), residual,
            gain.reshape(1, WIDTH), queries, keys,
        )

    inner = Mesh(mesh.devices.reshape(sizes), AXES)
    rows = ("zh", "y", "x")
    array = P(rows, "mp")
    return jax.shard_map(
        local, mesh=inner,
        in_specs=(array, array, array, P("mp", None), P("mp"), array, P("mp"), array, array),
        out_specs=(array, array), check_vma=False,
    )


def solution(mesh):
    seq, nm = mesh.shape["seq"], mesh.shape["mp"]
    return build(mesh, (2, seq // 8, 4, nm))
```
